256 devices in a mesh: gy: 16 (over z, y_lo), gz: 16 (over y_hi, x, core).
Axes of the slice: x: 4, y: 4 (y_hi: 2, y_lo: 2; y = y_hi * 2 + y_lo), z: 8, core: 2. Of those that a mesh axis runs over, the one named last changes fastest.
Arguments:
- velocity: float32 [3, 128, 128, 512], P(None, 'gy', 'gz'), may hold values from -6 to 6
- forcing: float32 [3, 128, 128, 512], P(None, 'gy', 'gz'), may hold values from -1.5 to 1.5, as said below
- first_kernel: bfloat16 [16, 3, 3, 3, 3], replicated, may hold values from -0.625 to 0.625
- first_bias: float32 [16], replicated, may hold values from -3 to 3
- second_kernel: bfloat16 [9, 16, 3, 3, 3], replicated, may hold values from -0.3125 to 0.3125
Outputs:
- velocity_next: float32 [3, 128, 128, 512], P(None, 'gy', 'gz')
The draws below stay inside these ranges and needn't reach their ends.
Inputs may be any that keep to these rules, and one draw needn't show every extreme that they name: forcing increment of one step.
All inputs are finite; a program needn't handle non-finite values.
Results may differ from the reference program's by a relative error of at most 0.0028.
Values may be sent and summed in bfloat16 or wider, within the bound.
A program may use at most 64 MiB of HBM per device.

```python
import math
import jax
import jax.numpy as jnp
from jax import lax

NX = 512
HID = 16
NY = 128
NZ = 128


def draw_forcing(key, part):
    increment = jnp.clip(jax.random.normal(key, (3, NY, NZ, NX), jnp.float32) * 0.3, -1.5, 1.5)
    return increment


def block_levels(stream_key, dims, pieces, low, high):
    level, own = 1.0, jax.random.fold_in(stream_key, 6)
    for axis_at, blocks in pieces:
        heights = jnp.exp(jax.random.uniform(jax.random.fold_in(own, axis_at), (blocks,), jnp.float32, low / len(pieces), high / len(pieces)))
        level = level * jnp.repeat(heights, dims[axis_at] // blocks).reshape([-1 if axis == axis_at else 1 for axis in range(len(dims))])
    return level


def centred(rng, shape, spread, reach, shards=(), kind=jnp.bfloat16):
    level = block_levels(rng, shape, shards, -0.22, 0.18) if shards else 1.0
    values = jax.random.normal(rng, shape, jnp.float32) * spread * level
    return jnp.minimum(jnp.maximum(values, -reach), reach).astype(kind)


def setup_inputs(seed: int = 0) -> dict:
    seeds = jax.random.split(jax.random.key(seed), 6)
    return {
        "velocity": centred(seeds[0], (3, NY, NZ, NX), 1.0, 6.0, ((1, 16), (2, 16)), jnp.float32),
        "forcing": draw_forcing(jax.random.fold_in(seeds[5], 71), 0),
        "first_kernel": centred(seeds[2], (HID, 3, 3, 3, 3), 81 ** -0.5, 0.625),
        "first_bias": centred(seeds[3], (HID,), 0.5, 3.0, (), jnp.float32),
        "second_kernel": centred(seeds[4], (9, HID, 3, 3, 3), (27 * HID) ** -0.5, 0.3125),
    }


time_step = 0.02
viscosity = 0.002


def periodic_convolution(source, kernel):
    padded = jnp.pad(source, ((0, 0), (1, 1), (1, 1), (1, 1)), mode="wrap")
    result = lax.conv_general_dilated(padded[None], kernel, (1, 1, 1), "VALID", dimension_numbers=("NCDHW", "OIDHW", "NCDHW"), precision=lax.Precision.HIGHEST)
    return result[0]


def signed_waves(extent):
    indices = jnp.arange(extent, dtype=jnp.int32)
    waves = jnp.where(2 * indices > extent, indices - extent, indices)
    waves = jnp.where(2 * indices == extent, 0, waves)
    return waves.astype(jnp.float32)


def reference(velocity, forcing, first_kernel, first_bias, second_kernel):
    rounded = lax.optimization_barrier(velocity.astype(jnp.bfloat16))
    before = periodic_convolution(rounded.astype(jnp.float32), first_kernel.astype(jnp.float32)) + first_bias[:, None, None, None]
    hidden = lax.optimization_barrier(jax.nn.silu(before).astype(jnp.bfloat16))
    learned = periodic_convolution(hidden.astype(jnp.float32), second_kernel.astype(jnp.float32)).astype(jnp.bfloat16)
    learned = lax.optimization_barrier(learned).astype(jnp.float32).reshape(3, 3, NY, NZ, NX)
    spacings = (2.0 * math.pi / NX, 2.0 * math.pi / NY, 2.0 * math.pi / NZ)
    axes_of = (3, 1, 2)
    divergence = jnp.zeros_like(velocity)
    laplacian = jnp.zeros_like(velocity)
    for direction in range(3):
        array_axis = axes_of[direction]
        fluxes = velocity * velocity[direction] + learned[:, direction]
        divergence = divergence + (jnp.roll(fluxes, -1, array_axis) - jnp.roll(fluxes, 1, array_axis)) / (2.0 * spacings[direction])
        laplacian = laplacian + (jnp.roll(velocity, -1, array_axis) + jnp.roll(velocity, 1, array_axis) - 2.0 * velocity) / spacings[direction] ** 2
    stepped = velocity + time_step * (viscosity * laplacian - divergence) + forcing
    spectrum = jnp.fft.fftn(stepped, axes=(1, 2, 3))
    row_waves = signed_waves(NY)[:, None, None]
    depth_waves = signed_waves(NZ)[None, :, None]
    line_waves = signed_waves(NX)[None, None, :]
    squared = line_waves ** 2 + row_waves ** 2 + depth_waves ** 2
    inverse_square = jnp.where(squared > 0, 1.0 / jnp.maximum(squared, 1.0), 0.0)
    potential = (line_waves * spectrum[0] + row_waves * spectrum[1] + depth_waves * spectrum[2]) * inverse_square
    projected = spectrum - jnp.stack([line_waves * potential, row_waves * potential, depth_waves * potential])
    return jnp.real(jnp.fft.ifftn(projected, axes=(1, 2, 3))).astype(jnp.float32)
```

```python
from functools import reduce
import math

import jax
import jax.numpy as jnp
import numpy as np
from jax import lax
from jax.experimental import pallas as pl
from jax.experimental.pallas import tpu as pltpu
from jax.sharding import PartitionSpec as P

time_step = 0.02
viscosity = 0.002
highest = lax.Precision.HIGHEST


def extended_2(block, sides, width):
    for axis, dim in sides:
        count = lax.axis_size(axis)
        forward = [(i, i + 1) for i in range(count - 1)]
        forward.append((count - 1, 0))
        backward = [(target, source) for source, target in forward]
        low = lax.ppermute(
            lax.slice_in_dim(block, block.shape[dim] - width, None, axis=dim), axis, forward
        )
        high = lax.ppermute(lax.slice_in_dim(block, 0, width, axis=dim), axis, backward)
        block = jnp.concatenate([low, block, high], axis=dim)
    return block


MESH = pl.DeviceIdType.MESH
BF = jnp.bfloat16
F32 = jnp.float32
GY, GZ = 16, 16
PEERS = GY * GZ
NL = 512
CELLS = 64


def halves(table):
    high = table.astype(BF)
    low = (table - high.astype(np.float64)).astype(BF)
    return high, low


def root_tables(size):
    index = np.arange(size)
    angle = 2.0 * np.pi * (np.outer(index, index) % size) / size
    return np.cos(angle), np.sin(angle)


def spectral_tables():
    mode = np.arange(PEERS)
    cell = np.arange(NL)
    angle = 2.0 * np.pi * (np.outer(mode, cell) % NL) / NL
    real, imag = np.cos(angle), -np.sin(angle)
    imag[0] = 1.0 - 2.0 * (cell % 2)
    lines = np.concatenate([real, imag], axis=0)
    cos16, sin16 = root_tables(16)
    wide_cos = np.kron(cos16, cos16) - np.kron(sin16, sin16)
    wide_sin = np.kron(sin16, cos16) + np.kron(cos16, sin16)
    outer = np.concatenate([wide_cos, wide_sin], axis=0)
    cos8, sin8 = root_tables(8)
    near_cos = np.kron(cos8, cos8) - np.kron(sin8, sin8)
    near_sin = np.kron(sin8, cos8) + np.kron(cos8, sin8)
    inner = np.block([[near_cos, -near_sin], [near_sin, near_cos]])
    row = np.arange(PEERS)
    lane = np.arange(2 * CELLS)
    first = np.outer(row // GZ, (lane % CELLS) // 8)
    second = np.outer(row % GZ, lane % 8)
    turn = 2.0 * np.pi * ((first + second) % 128) / 128
    sign = np.where(lane < CELLS, 1.0, -1.0)[None, :]
    twiddle = np.stack([np.cos(turn), np.sin(turn) * sign]).astype(np.float32)

    def signed(index):
        wave = np.where(2 * index > 128, index - 128, index)
        return np.where(2 * index == 128, 0, wave)

    wave_y = signed((row // GZ)[:, None] + 16 * ((lane % CELLS) // 8)[None, :])
    wave_z = signed((row % GZ)[:, None] + 16 * (lane % 8)[None, :])
    waves = np.stack([wave_y, wave_z]).astype(np.float32)
    return (*halves(lines), *halves(outer), *halves(inner), *halves(inner.T.copy()), twiddle, waves)


def split(value):
    high = value.astype(BF)
    return high, (value - high.astype(F32)).astype(BF)


def dot(left, right, dims=((1,), (0,))):
    return lax.dot_general(left, right, (dims, ((), ())), preferred_element_type=F32)


def enter(ready):
    gy, gz = lax.axis_index("gy"), lax.axis_index("gz")
    barrier = pltpu.get_barrier_semaphore()

    def greet(step, carry):
        pl.semaphore_signal(barrier, inc=1, device_id=(lax.rem(gy + step, GY), gz), device_id_type=MESH)
        pl.semaphore_signal(barrier, inc=1, device_id=(gy, lax.rem(gz + step, GZ)), device_id_type=MESH)
        return carry

    lax.fori_loop(1, 16, greet, 0)
    pl.semaphore_wait(barrier, GY + GZ - 2)

    def confirm(step, carry):
        pl.semaphore_signal(ready, inc=1, device_id=(gy, lax.rem(gz + step, GZ)), device_id_type=MESH)
        return carry

    lax.fori_loop(1, GZ, confirm, 0)
    pl.semaphore_wait(ready, GZ - 1)


def exchange(source, target, send_sem, recv_sem, own_sem):
    gy, gz = lax.axis_index("gy"), lax.axis_index("gz")
    me = gy * GZ + gz

    def send(step, carry):
        ty, tz = lax.rem(gy + lax.rem(step, GY), GY), lax.rem(gz + step // GY, GZ)
        pltpu.make_async_remote_copy(
            source.at[ty * GZ + tz],
            target.at[me],
            send_sem,
            recv_sem,
            device_id=(ty, tz),
            device_id_type=MESH,
        ).start()
        return carry

    lax.fori_loop(1, PEERS, send, 0)
    own = pltpu.make_async_copy(source.at[me], target.at[me], own_sem)
    own.start()
    own.wait()
    others = pl.ds(0, PEERS - 1)
    pltpu.make_async_copy(source.at[others], target.at[others], recv_sem).wait()
    pltpu.make_async_copy(source.at[others], target.at[others], send_sem).wait()


def pack(parts, staged, outgoing):
    rest = parts[0] - parts[0].astype(BF).astype(F32)
    for row, part in enumerate((*parts, rest)):
        staged[pl.ds(row, PEERS, stride=4), :] = part
    outgoing[...] = staged[...].astype(BF).reshape(PEERS, 4, 128)


def unpack(incoming, staged):
    staged[...] = incoming[...].astype(F32).reshape(PEERS * 4, 128)
    return [staged[pl.ds(row, PEERS, stride=4), :].astype(BF) for row in range(4)]


def swapped(value):
    return pltpu.roll(value, CELLS, axis=1)


def spectral(
    stepped,
    lines_high,
    lines_low,
    outer_high,
    outer_low,
    inner_high,
    inner_low,
    back_high,
    back_low,
    twiddle,
    waves,
    result,
    staged,
    outgoing,
    incoming,
    outgoing_back,
    incoming_back,
    sems,
    ready,
):
    enter(ready)
    gy, gz = lax.axis_index("gy"), lax.axis_index("gz")
    nt = ((1,), (1,))
    high, low = split(stepped[...].reshape(3 * CELLS, NL))
    modes = dot(lines_high[...], high, nt) + (dot(lines_low[...], high, nt) + dot(lines_high[...], low, nt))
    pack(
        [
            jnp.concatenate(
                [modes[:PEERS, CELLS * c : CELLS * (c + 1)], modes[PEERS:, CELLS * c : CELLS * (c + 1)]],
                axis=1,
            )
            for c in range(3)
        ],
        staged,
        outgoing,
    )
    exchange(outgoing, incoming, sems.at[0], sems.at[1], sems.at[2])
    rows = jnp.concatenate(unpack(incoming, staged), axis=1)
    both = dot(outer_high[...], rows) + dot(outer_low[...], rows)
    lane = lax.broadcasted_iota(jnp.int32, (PEERS, 128), 1)
    sign = jnp.where(lane < CELLS, 1.0, -1.0).astype(F32)
    spun = []
    for c in range(3):
        at = 128 * c
        upper, lower = both[:PEERS, at : at + 128], both[PEERS:, at : at + 128]
        if c == 0:
            upper, lower = upper + both[:PEERS, 384:], lower + both[PEERS:, 384:]
        value = upper + swapped(lower) * sign
        spun.append(value * twiddle[0] + swapped(value) * twiddle[1])
    high, low = split(jnp.concatenate(spun, axis=0))
    modes = dot(high, inner_high[...]) + (dot(low, inner_high[...]) + dot(high, inner_low[...]))
    slot = gy * GZ + gz
    wave_x = slot.astype(F32)
    wave_y, wave_z = waves[0], waves[1]
    squared = wave_x * wave_x + wave_y * wave_y + wave_z * wave_z
    inverse = jnp.where(squared > 0, 1.0 / jnp.maximum(squared, 1.0), 0.0)
    parts = [modes[PEERS * c : PEERS * (c + 1)] for c in range(3)]
    potential = (wave_x * parts[0] + wave_y * parts[1] + wave_z * parts[2]) * inverse
    weight = jnp.where(slot == 0, 1.0, 2.0).astype(F32) / (NL * 128.0 * 128.0)
    parts = [
        (part - wave * potential) * weight for part, wave in zip(parts, (wave_x, wave_y, wave_z))
    ]
    high, low = split(jnp.concatenate(parts, axis=0))
    near = dot(high, back_high[...]) + (dot(low, back_high[...]) + dot(high, back_low[...]))
    spun = []
    for c in range(3):
        value = near[PEERS * c : PEERS * (c + 1)]
        spun.append(value * twiddle[0] - swapped(value) * twiddle[1])
    high, low = split(jnp.concatenate(spun, axis=1))
    both = dot(outer_high[...], high) + (dot(outer_high[...], low) + dot(outer_low[...], high))
    pack(
        [
            both[:PEERS, 128 * c : 128 * (c + 1)] - swapped(both[PEERS:, 128 * c : 128 * (c + 1)]) * sign
            for c in range(3)
        ],
        staged,
        outgoing_back,
    )
    exchange(outgoing_back, incoming_back, sems.at[3], sems.at[4], sems.at[5])
    rows = [value.astype(F32) for value in unpack(incoming_back, staged)]
    real = jnp.concatenate([value[:, :CELLS] for value in rows], axis=1)
    imag = jnp.concatenate([value[:, CELLS:] for value in rows], axis=1)
    packed = jnp.concatenate([real, imag], axis=0).T.astype(BF)
    field = dot(packed, lines_high[...]) + dot(packed, lines_low[...])
    result[...] = jnp.concatenate(
        [field[:CELLS] + field[3 * CELLS :], field[CELLS : 3 * CELLS]], axis=0
    ).reshape(3, CELLS, NL)


def project(stepped, row_devices, depth_devices):
    tables = spectral_tables()
    vmem = pl.BlockSpec(memory_space=pltpu.VMEM)
    return pl.pallas_call(
        spectral,
        out_shape=jax.ShapeDtypeStruct(stepped.shape, F32),
        in_specs=[vmem] * (1 + len(tables)),
        out_specs=vmem,
        scratch_shapes=[
            pltpu.VMEM((4 * PEERS, 128), F32),
            *[pltpu.VMEM((PEERS, 4, 128), BF)] * 4,
            pltpu.SemaphoreType.DMA((6,)),
            pltpu.SemaphoreType.REGULAR,
        ],
        compiler_params=pltpu.CompilerParams(
            collective_id=0, has_side_effects=True, vmem_limit_bytes=48 * 2**20
        ),
    )(stepped, *tables)


def periodic_convolution(source, weight):
    channels = source.shape[0]
    inner_rows = source.shape[1] - 2
    inner_depth = source.shape[2] - 2
    stacked = jnp.concatenate([jnp.roll(source, 1 - offset, axis=3) for offset in range(3)], axis=0)
    matrices = jnp.transpose(weight, (0, 2, 3, 4, 1)).reshape(weight.shape[0], 3, 3, 3 * channels)
    partial_sums = []
    for first_shift in range(3):
        for second_shift in range(3):
            window = stacked[
                :,
                first_shift : first_shift + inner_rows,
                second_shift : second_shift + inner_depth,
                :,
            ]
            partial_sums.append(
                jnp.einsum(
                    "ok,kyzx->oyzx",
                    matrices[:, first_shift, second_shift],
                    window,
                    preferred_element_type=jnp.float32,
                )
            )
    return reduce(jnp.add, partial_sums)


def tendency(extended, learned_first, learned_rest, spacings):
    center = extended[:, 1:-1, 1:-1]
    flux_first = center * center[0:1] + learned_first
    divergence = (jnp.roll(flux_first, -1, axis=3) - jnp.roll(flux_first, 1, axis=3)) / (
        2.0 * spacings[0]
    )
    column = extended[:, :, 1:-1]
    flux_second = column * column[1:2] + learned_rest[:, 0, :, 1:-1]
    divergence = divergence + (flux_second[:, 2:] - flux_second[:, :-2]) / (2.0 * spacings[1])
    planes = extended[:, 1:-1, :]
    flux_third = planes * planes[2:3] + learned_rest[:, 1, 1:-1, :]
    divergence = divergence + (flux_third[:, :, 2:] - flux_third[:, :, :-2]) / (2.0 * spacings[2])
    laplacian = (
        jnp.roll(center, -1, axis=3) + jnp.roll(center, 1, axis=3) - 2.0 * center
    ) / spacings[0] ** 2
    laplacian = (
        laplacian
        + (extended[:, 2:, 1:-1] + extended[:, :-2, 1:-1] - 2.0 * center) / spacings[1] ** 2
    )
    laplacian = (
        laplacian
        + (extended[:, 1:-1, 2:] + extended[:, 1:-1, :-2] - 2.0 * center) / spacings[2] ** 2
    )
    return viscosity * laplacian - divergence


def body(velocity, forcing, first_kernel, first_bias, second_kernel):
    row_devices = lax.axis_size("gy")
    depth_devices = lax.axis_size("gz")
    local_rows = velocity.shape[1]
    local_depth = velocity.shape[2]
    line_cells = velocity.shape[3]
    all_rows = local_rows * row_devices
    all_depth = local_depth * depth_devices
    spacings = (2.0 * math.pi / line_cells, 2.0 * math.pi / all_rows, 2.0 * math.pi / all_depth)
    bias_column = first_bias[:, None, None, None]
    extended = extended_2(velocity, (("gy", 1), ("gz", 2)), 1)
    hidden = jax.nn.silu(
        periodic_convolution(extended.astype(jnp.bfloat16), first_kernel) + bias_column
    ).astype(jnp.bfloat16)
    hidden_wide = extended_2(hidden, (("gy", 1), ("gz", 2)), 1)
    correction = periodic_convolution(hidden_wide, second_kernel).astype(jnp.bfloat16)
    correction = correction.reshape(3, 3, local_rows, local_depth, line_cells)
    learned_first = correction[:, 0]
    learned_rest = extended_2(correction[:, 1:], (("gy", 2), ("gz", 3)), 1)
    stepped = (
        velocity + time_step * tendency(extended, learned_first, learned_rest, spacings) + forcing
    )
    projected = project(stepped.reshape(3, local_rows * local_depth, line_cells), row_devices, depth_devices)
    return projected.reshape(stepped.shape)


def solution(mesh):
    placed = (P(None, "gy", "gz", None), P(None, "gy", "gz", None), P(), P(), P())
    return jax.shard_map(
        body, mesh=mesh, in_specs=placed, out_specs=P(None, "gy", "gz", None), check_vma=False
    )
```

```python
import math

import jax
import jax.numpy as jnp
import numpy as np
from jax import lax
from jax.experimental import pallas as pl
from jax.experimental.pallas import tpu as pltpu
from jax.sharding import PartitionSpec as P

time_step = 0.02
viscosity = 0.002
MESH = pl.DeviceIdType.MESH
BF = jnp.bfloat16
F32 = jnp.float32
GY, GZ = 16, 16
PEERS = GY * GZ
NL = 512
CELLS = 64


def halves(table):
    high = table.astype(BF)
    low = (table - high.astype(np.float64)).astype(BF)
    return high, low


def root_tables(size):
    index = np.arange(size)
    angle = 2.0 * np.pi * (np.outer(index, index) % size) / size
    return np.cos(angle), np.sin(angle)


def spectral_tables():
    mode = np.arange(PEERS)
    cell = np.arange(NL)
    angle = 2.0 * np.pi * (np.outer(mode, cell) % NL) / NL
    real, imag = np.cos(angle), -np.sin(angle)
    imag[0] = 1.0 - 2.0 * (cell % 2)
    lines = np.concatenate([real, imag], axis=0)
    cos16, sin16 = root_tables(16)
    wide_cos = np.kron(cos16, cos16) - np.kron(sin16, sin16)
    wide_sin = np.kron(sin16, cos16) + np.kron(cos16, sin16)
    outer = np.concatenate([wide_cos, wide_sin], axis=0)
    cos8, sin8 = root_tables(8)
    near_cos = np.kron(cos8, cos8) - np.kron(sin8, sin8)
    near_sin = np.kron(sin8, cos8) + np.kron(cos8, sin8)
    inner = np.block([[near_cos, -near_sin], [near_sin, near_cos]])
    row = np.arange(PEERS)
    lane = np.arange(2 * CELLS)
    first = np.outer(row // GZ, (lane % CELLS) // 8)
    second = np.outer(row % GZ, lane % 8)
    turn = 2.0 * np.pi * ((first + second) % 128) / 128
    sign = np.where(lane < CELLS, 1.0, -1.0)[None, :]
    twiddle = np.stack([np.cos(turn), np.sin(turn) * sign]).astype(np.float32)

    def signed(index):
        wave = np.where(2 * index > 128, index - 128, index)
        return np.where(2 * index == 128, 0, wave)

    wave_y = signed((row // GZ)[:, None] + 16 * ((lane % CELLS) // 8)[None, :])
    wave_z = signed((row % GZ)[:, None] + 16 * (lane % 8)[None, :])
    waves = np.stack([wave_y, wave_z]).astype(np.float32)
    return (*halves(lines), *halves(outer), *halves(inner), *halves(inner.T.copy()), twiddle, waves)


def split(value):
    high = value.astype(BF)
    return high, (value - high.astype(F32)).astype(BF)


def dot(left, right, dims=((1,), (0,))):
    return lax.dot_general(left, right, (dims, ((), ())), preferred_element_type=F32)


def greet_all():
    gy, gz = lax.axis_index("gy"), lax.axis_index("gz")
    barrier = pltpu.get_barrier_semaphore()

    def greet(step, carry):
        pl.semaphore_signal(barrier, inc=1, device_id=(lax.rem(gy + step, GY), gz), device_id_type=MESH)
        pl.semaphore_signal(barrier, inc=1, device_id=(gy, lax.rem(gz + step, GZ)), device_id_type=MESH)
        return carry

    lax.fori_loop(1, 16, greet, 0)


def meet_all(ready):
    gy, gz = lax.axis_index("gy"), lax.axis_index("gz")
    pl.semaphore_wait(pltpu.get_barrier_semaphore(), GY + GZ - 2)

    def confirm(step, carry):
        pl.semaphore_signal(ready, inc=1, device_id=(gy, lax.rem(gz + step, GZ)), device_id_type=MESH)
        return carry

    lax.fori_loop(1, GZ, confirm, 0)
    pl.semaphore_wait(ready, GZ - 1)


def exchange(source, target, send_sem, recv_sem, own_sem):
    gy, gz = lax.axis_index("gy"), lax.axis_index("gz")
    me = gy * GZ + gz

    def send(step, carry):
        ty, tz = lax.rem(gy + lax.rem(step, GY), GY), lax.rem(gz + step // GY, GZ)
        pltpu.make_async_remote_copy(
            source.at[ty * GZ + tz],
            target.at[me],
            send_sem,
            recv_sem,
            device_id=(ty, tz),
            device_id_type=MESH,
        ).start()
        return carry

    lax.fori_loop(1, PEERS, send, 0)
    own = pltpu.make_async_copy(source.at[me], target.at[me], own_sem)
    own.start()
    own.wait()
    others = pl.ds(0, PEERS - 1)
    pltpu.make_async_copy(source.at[others], target.at[others], recv_sem).wait()
    pltpu.make_async_copy(source.at[others], target.at[others], send_sem).wait()


def pack(parts, staged, outgoing):
    rest = parts[0] - parts[0].astype(BF).astype(F32)
    for row, part in enumerate((*parts, rest)):
        staged[pl.ds(row, PEERS, stride=4), :] = part
    outgoing[...] = staged[...].astype(BF).reshape(PEERS, 4, 128)


def unpack(incoming, staged):
    staged[...] = incoming[...].astype(F32).reshape(PEERS * 4, 128)
    return [staged[pl.ds(row, PEERS, stride=4), :].astype(BF) for row in range(4)]


def swapped(value):
    return pltpu.roll(value, CELLS, axis=1)


WIDE = 14
SPAN = 3 * 4 * WIDE
HIDDEN = 16


def neighbours():
    return [(a, b) for a in (-1, 0, 1) for b in (-1, 0, 1) if (a, b) != (0, 0)]


def span(side, sending):
    if side == 0:
        return pl.ds(0, 8) if sending else pl.ds(3, 8)
    if side < 0:
        return pl.ds(0, 3) if sending else pl.ds(WIDE - 3, 3)
    return pl.ds(5, 3) if sending else pl.ds(0, 3)


def halo(edge, around, sems):
    gy, gz = lax.axis_index("gy"), lax.axis_index("gz")
    copies = []
    for index, (a, b) in enumerate(neighbours()):
        copies.append(
            pltpu.make_async_remote_copy(
                edge.at[span(a, True), span(b, True)],
                around.at[span(a, False), span(b, False)],
                sems.at[index],
                sems.at[8 + index],
                device_id=(lax.rem(gy + a + GY, GY), lax.rem(gz + b + GZ, GZ)),
                device_id_type=MESH,
            )
        )
    for copy in copies:
        copy.start()
    return copies


def taken(cells, y, rows):
    return jnp.concatenate([cells[y, t, rows, :] for t in range(4)], axis=1)


def put(cells, y, rows, value):
    for t in range(4):
        cells[y, t, rows, :] = value[:, 128 * t : 128 * (t + 1)]


def prepare(velocity, first, second, cells, edge, first_matrix, second_rows, second_matrix):
    def place(y, carry):
        for c in range(4):
            value = velocity[c, y] if c < 3 else jnp.zeros((8, NL), F32)
            for t in range(4):
                cells[y + 3, t, pl.ds(12 + c, 8, stride=4), :] = value[:, 128 * t : 128 * (t + 1)]
        edge[y] = taken(cells, y + 3, pl.ds(12, 32)).astype(BF).reshape(8, 4, NL)
        return carry

    lax.fori_loop(0, 8, place, 0)
    for z in range(12):
        rows = first[...] if z == 0 else pltpu.roll(first[...], 4 * z, axis=1)
        first_matrix[pl.ds(HIDDEN * z, HIDDEN), :] = rows.astype(BF)
    for z in range(8):
        rows = second[...] if z == 0 else pltpu.roll(second[...], HIDDEN * z, axis=1)
        for t in range(5):
            second_rows[t, pl.ds(z, 27, stride=8), :] = rows[:27, 128 * t : 128 * (t + 1)]
    second_matrix[...] = jnp.concatenate([second_rows[t] for t in range(5)], axis=1)[:, : 36 * HIDDEN].astype(BF)


def spread(around, cells, stacked):
    for y in (*range(3), *range(WIDE - 3, WIDE)):
        put(cells, y, pl.ds(0, 4 * WIDE), around[y].astype(F32).reshape(4 * WIDE, NL))

    def sides(y, carry):
        put(cells, y, pl.ds(0, 12), around[y, pl.ds(0, 3)].astype(F32).reshape(12, NL))
        put(cells, y, pl.ds(44, 12), around[y, pl.ds(11, 3)].astype(F32).reshape(12, NL))
        return carry

    lax.fori_loop(3, 11, sides, 0)

    def stack(y, carry):
        row = taken(cells, y, pl.ds(0, 4 * WIDE))
        at = y * SPAN
        stacked[pl.ds(pl.multiple_of(at, 8), 56), :] = pltpu.roll(row, 1, axis=1)
        stacked[pl.ds(pl.multiple_of(at + 56, 8), 56), :] = row
        stacked[pl.ds(pl.multiple_of(at + 112, 8), 56), :] = pltpu.roll(row, NL - 1, axis=1)
        return carry

    lax.fori_loop(0, WIDE, stack, 0)
    stacked[pl.ds(WIDE * SPAN, 8), :] = jnp.zeros((8, NL), F32)


def correct(bias, stacked, first_matrix, second_matrix, learned):
    learned[0] = jnp.zeros((72, NL), F32)
    learned[1] = jnp.zeros((72, NL), F32)

    def layer(y, carry):
        source = stacked[pl.ds(pl.multiple_of(y * SPAN, 8), 512), :].astype(BF)
        before = dot(first_matrix[...], source) + bias[...]
        hidden = before * (0.5 + 0.5 * jnp.tanh(0.5 * before))
        wide = jnp.concatenate(
            [
                pltpu.roll(hidden, 1, axis=1).astype(BF),
                hidden.astype(BF),
                pltpu.roll(hidden, NL - 1, axis=1).astype(BF),
            ],
            axis=0,
        )
        part = dot(second_matrix[...], wide)
        learned[y + 2] = part[:72]
        learned[y + 1] += part[72:144]
        learned[y] += part[144:]
        return carry

    lax.fori_loop(0, 12, layer, 0)


def advance(velocity, forcing, cells, learned, stepped):
    steps = (2.0 * math.pi / NL, 2.0 * math.pi / 128, 2.0 * math.pi / 128)
    half = [0.5 / h for h in steps]
    square = [1.0 / h**2 for h in steps]

    def ahead(value):
        return pltpu.roll(value, NL - 1, axis=1)

    def behind(value):
        return pltpu.roll(value, 1, axis=1)

    def lines(y, c, z):
        return taken(cells, y, pl.ds(12 + 4 * z + c, 8, stride=4))

    def move(y, carry):
        here = [velocity[c, y] for c in range(3)]
        over = [lines(y + 4, c, 0) for c in range(3)]
        under = [lines(y + 2, c, 0) for c in range(3)]
        far = [lines(y + 3, c, 1) for c in range(3)]
        near = [lines(y + 3, c, -1) for c in range(3)]
        for i in range(3):
            first = here[i] * here[0] + learned[y + 3, pl.ds(8 * i, 8), :].astype(BF).astype(F32)
            rows = pl.ds(24 + 8 * i, 8)
            second = (over[i] * over[1] + learned[y + 4, rows, :]) - (
                under[i] * under[1] + learned[y + 2, rows, :]
            )
            third = (far[i] * far[2] - near[i] * near[2]) + learned[y + 3, pl.ds(48 + 8 * i, 8), :]
            divergence = (
                (ahead(first) - behind(first)) * half[0] + second * half[1] + third * half[2]
            )
            twice = 2.0 * here[i]
            laplacian = (
                (ahead(here[i]) + behind(here[i]) - twice) * square[0]
                + (over[i] + under[i] - twice) * square[1]
                + (far[i] + near[i] - twice) * square[2]
            )
            stepped[i, pl.ds(pl.multiple_of(8 * y, 8), 8), :] = (
                here[i] + time_step * (viscosity * laplacian - divergence) + forcing[i, y]
            )
        return carry

    lax.fori_loop(0, 8, move, 0)


def first_rows(kernel):
    rows = jnp.transpose(kernel, (0, 2, 4, 3, 1)).astype(F32)
    rows = jnp.pad(rows, ((0, 0), (0, 0), (0, 0), (0, WIDE - 3), (0, 1)))
    return jnp.pad(rows.reshape(HIDDEN, 9 * 4 * WIDE), ((0, 0), (0, 8)))


def second_rows_of(kernel):
    taps = kernel.astype(F32).reshape(3, 3, HIDDEN, 3, 3, 3)
    taps = jnp.transpose(taps, (3, 1, 0, 5, 4, 2))
    quiet = ((0, 0),) * 4
    middle = jnp.pad(taps[:, :2], (*quiet, (1, 1), (0, 0)))
    slope = jnp.pad(taps[:, 2:], (*quiet, (2, 0), (0, 0))) - jnp.pad(taps[:, 2:], (*quiet, (0, 2), (0, 0)))
    rows = jnp.concatenate([middle, slope], axis=1)
    rows = jnp.pad(rows, (*quiet, (0, 7), (0, 0))).reshape(27, 36 * HIDDEN)
    return jnp.pad(rows, ((0, 5), (0, 4 * HIDDEN)))


def whole(
    velocity,
    forcing,
    first,
    bias,
    second,
    lines_high,
    lines_low,
    outer_high,
    outer_low,
    inner_high,
    inner_low,
    back_high,
    back_low,
    twiddle,
    waves,
    result,
    cells,
    edge,
    around,
    stacked,
    first_matrix,
    second_rows,
    second_matrix,
    learned,
    stepped,
    staged,
    outgoing,
    incoming,
    outgoing_back,
    incoming_back,
    halo_sems,
    sems,
    ready,
):
    greet_all()
    prepare(velocity, first, second, cells, edge, first_matrix, second_rows, second_matrix)
    meet_all(ready)
    copies = halo(edge, around, halo_sems)
    for copy in copies:
        copy.wait()
    spread(around, cells, stacked)
    correct(bias, stacked, first_matrix, second_matrix, learned)
    advance(velocity, forcing, cells, learned, stepped)
    gy, gz = lax.axis_index("gy"), lax.axis_index("gz")
    nt = ((1,), (1,))
    high, low = split(stepped[...].reshape(3 * CELLS, NL))
    modes = dot(lines_high[...], high, nt) + (dot(lines_low[...], high, nt) + dot(lines_high[...], low, nt))
    pack(
        [
            jnp.concatenate(
                [modes[:PEERS, CELLS * c : CELLS * (c + 1)], modes[PEERS:, CELLS * c : CELLS * (c + 1)]],
                axis=1,
            )
            for c in range(3)
        ],
        staged,
        outgoing,
    )
    exchange(outgoing, incoming, sems.at[0], sems.at[1], sems.at[2])
    rows = jnp.concatenate(unpack(incoming, staged), axis=1)
    both = dot(outer_high[...], rows) + dot(outer_low[...], rows)
    lane = lax.broadcasted_iota(jnp.int32, (PEERS, 128), 1)
    sign = jnp.where(lane < CELLS, 1.0, -1.0).astype(F32)
    spun = []
    for c in range(3):
        at = 128 * c
        upper, lower = both[:PEERS, at : at + 128], both[PEERS:, at : at + 128]
        if c == 0:
            upper, lower = upper + both[:PEERS, 384:], lower + both[PEERS:, 384:]
        value = upper + swapped(lower) * sign
        spun.append(value * twiddle[0] + swapped(value) * twiddle[1])
    high, low = split(jnp.concatenate(spun, axis=0))
    modes = dot(high, inner_high[...]) + (dot(low, inner_high[...]) + dot(high, inner_low[...]))
    slot = gy * GZ + gz
    wave_x = slot.astype(F32)
    wave_y, wave_z = waves[0], waves[1]
    squared = wave_x * wave_x + wave_y * wave_y + wave_z * wave_z
    inverse = jnp.where(squared > 0, 1.0 / jnp.maximum(squared, 1.0), 0.0)
    parts = [modes[PEERS * c : PEERS * (c + 1)] for c in range(3)]
    potential = (wave_x * parts[0] + wave_y * parts[1] + wave_z * parts[2]) * inverse
    weight = jnp.where(slot == 0, 1.0, 2.0).astype(F32) / (NL * 128.0 * 128.0)
    parts = [
        (part - wave * potential) * weight for part, wave in zip(parts, (wave_x, wave_y, wave_z))
    ]
    high, low = split(jnp.concatenate(parts, axis=0))
    near = dot(high, back_high[...]) + (dot(low, back_high[...]) + dot(high, back_low[...]))
    spun = []
    for c in range(3):
        value = near[PEERS * c : PEERS * (c + 1)]
        spun.append(value * twiddle[0] - swapped(value) * twiddle[1])
    high, low = split(jnp.concatenate(spun, axis=1))
    both = dot(outer_high[...], high) + (dot(outer_high[...], low) + dot(outer_low[...], high))
    pack(
        [
            both[:PEERS, 128 * c : 128 * (c + 1)] - swapped(both[PEERS:, 128 * c : 128 * (c + 1)]) * sign
            for c in range(3)
        ],
        staged,
        outgoing_back,
    )
    exchange(outgoing_back, incoming_back, sems.at[3], sems.at[4], sems.at[5])
    rows = [value.astype(F32) for value in unpack(incoming_back, staged)]
    real = jnp.concatenate([value[:, :CELLS] for value in rows], axis=1)
    imag = jnp.concatenate([value[:, CELLS:] for value in rows], axis=1)
    packed = jnp.concatenate([real, imag], axis=0).T.astype(BF)
    field = dot(packed, lines_high[...]) + dot(packed, lines_low[...])
    result[...] = jnp.concatenate(
        [field[:CELLS] + field[3 * CELLS :], field[CELLS : 3 * CELLS]], axis=0
    ).reshape(3, CELLS, NL)


def body(velocity, forcing, first_kernel, first_bias, second_kernel):
    tables = spectral_tables()
    vmem = pl.BlockSpec(memory_space=pltpu.VMEM)
    bias = jnp.broadcast_to(first_bias[None, :], (12, HIDDEN)).reshape(12 * HIDDEN, 1)
    field = pl.pallas_call(
        whole,
        out_shape=jax.ShapeDtypeStruct((3, CELLS, NL), F32),
        in_specs=[vmem] * (5 + len(tables)),
        out_specs=vmem,
        scratch_shapes=[
            pltpu.VMEM((WIDE, 4, 4 * WIDE, 128), F32),
            pltpu.VMEM((8, 8, 4, NL), BF),
            pltpu.VMEM((WIDE, WIDE, 4, NL), BF),
            pltpu.VMEM((WIDE * SPAN + 8, NL), F32),
            pltpu.VMEM((12 * HIDDEN, 512), BF),
            pltpu.VMEM((5, 216, 128), F32),
            pltpu.VMEM((216, 36 * HIDDEN), BF),
            pltpu.VMEM((WIDE, 72, NL), F32),
            pltpu.VMEM((3, CELLS, NL), F32),
            pltpu.VMEM((4 * PEERS, 128), F32),
            *[pltpu.VMEM((PEERS, 4, 128), BF)] * 4,
            pltpu.SemaphoreType.DMA((16,)),
            pltpu.SemaphoreType.DMA((6,)),
            pltpu.SemaphoreType.REGULAR,
        ],
        compiler_params=pltpu.CompilerParams(
            collective_id=0, has_side_effects=True, vmem_limit_bytes=56 * 2**20
        ),
    )(velocity, forcing, first_rows(first_kernel), bias, second_rows_of(second_kernel), *tables)
    return field.reshape(velocity.shape)


def solution(mesh):
    placed = (P(None, "gy", "gz", None), P(None, "gy", "gz", None), P(), P(), P())
    return jax.shard_map(
        body, mesh=mesh, in_specs=placed, out_specs=P(None, "gy", "gz", None), check_vma=False
    )
```

```python
import math

import jax
import jax.numpy as jnp
import numpy as np
from jax import lax
from jax.experimental import pallas as pl
from jax.experimental.pallas import tpu as pltpu
from jax.sharding import PartitionSpec as P

time_step = 0.02
viscosity = 0.002
UNROLL_PLACE = 2
UNROLL_STACK = 2
UNROLL_LAYER = 2
FAR = (4, 3, 5, 2, 6, 1, 7, 0)
MESH = pl.DeviceIdType.MESH
BF = jnp.bfloat16
F32 = jnp.float32
GY, GZ = 16, 16
PEERS = GY * GZ
NL = 512
CELLS = 64


def halves(table):
    high = table.astype(BF)
    low = (table - high.astype(np.float64)).astype(BF)
    return high, low


def root_tables(size):
    index = np.arange(size)
    angle = 2.0 * np.pi * (np.outer(index, index) % size) / size
    return np.cos(angle), np.sin(angle)


def spectral_tables():
    mode = np.arange(PEERS)
    cell = np.arange(NL)
    angle = 2.0 * np.pi * (np.outer(mode, cell) % NL) / NL
    real, imag = np.cos(angle), -np.sin(angle)
    imag[0] = 1.0 - 2.0 * (cell % 2)
    lines = np.concatenate([real, imag], axis=0)
    cos16, sin16 = root_tables(16)
    wide_cos = np.kron(cos16, cos16) - np.kron(sin16, sin16)
    wide_sin = np.kron(sin16, cos16) + np.kron(cos16, sin16)
    outer = np.concatenate([wide_cos, wide_sin], axis=0)
    cos8, sin8 = root_tables(8)
    near_cos = np.kron(cos8, cos8) - np.kron(sin8, sin8)
    near_sin = np.kron(sin8, cos8) + np.kron(cos8, sin8)
    inner = np.block([[near_cos, -near_sin], [near_sin, near_cos]])
    row = np.arange(PEERS)
    lane = np.arange(2 * CELLS)
    first = np.outer(row // GZ, (lane % CELLS) // 8)
    second = np.outer(row % GZ, lane % 8)
    turn = 2.0 * np.pi * ((first + second) % 128) / 128
    sign = np.where(lane < CELLS, 1.0, -1.0)[None, :]
    twiddle = np.stack([np.cos(turn), np.sin(turn) * sign]).astype(np.float32)

    return (*halves(lines), *halves(outer), *halves(inner), *halves(inner.T.copy()), twiddle)


def signed_waves():
    row = lax.broadcasted_iota(jnp.int32, (PEERS, 128), 0)
    lane = lax.rem(lax.broadcasted_iota(jnp.int32, (PEERS, 128), 1), CELLS)

    def signed(index):
        wave = jnp.where(2 * index > 128, index - 128, index)
        return jnp.where(2 * index == 128, 0, wave).astype(F32)

    return signed(row // GZ + 16 * (lane // 8)), signed(lax.rem(row, GZ) + 16 * lax.rem(lane, 8))


def split(value):
    high = value.astype(BF)
    return high, (value - high.astype(F32)).astype(BF)


def dot(left, right, dims=((1,), (0,))):
    return lax.dot_general(left, right, (dims, ((), ())), preferred_element_type=F32)


def shifted(a, b):
    gy, gz = lax.axis_index("gy"), lax.axis_index("gz")
    return (lax.rem(gy + a + GY, GY), lax.rem(gz + b + GZ, GZ))


def tell(sem, reach):
    for a, b in neighbours():
        pl.semaphore_signal(sem, inc=1, device_id=shifted(reach * a, reach * b), device_id_type=MESH)


def exchange(source, target, send_sem, recv_sem, own_sem):
    gy, gz = lax.axis_index("gy"), lax.axis_index("gz")
    me = gy * GZ + gz
    own = pltpu.make_async_copy(source.at[me], target.at[me], own_sem)
    own.start()
    own.wait()
    z, y_low = gy // 2, lax.rem(gy, 2)
    y_high, x, core = gz // 8, lax.rem(gz // 2, 4), lax.rem(gz, 2)
    for far in FAR:

        def send(step, carry):
            ty = lax.rem(z + far, 8) * 2 + lax.rem(y_low + lax.rem(step, 2), 2)
            tz = (
                lax.rem(y_high + lax.rem(step // 2, 2), 2) * 8
                + lax.rem(x + lax.rem(step // 4, 4), 4) * 2
                + lax.rem(core + step // 16, 2)
            )
            pltpu.make_async_remote_copy(
                source.at[ty * GZ + tz],
                target.at[me],
                send_sem,
                recv_sem,
                device_id=(ty, tz),
                device_id_type=MESH,
            ).start()
            return carry

        lax.fori_loop(0 if far else 1, 32, send, 0)
    others = pl.ds(0, PEERS - 1)
    pltpu.make_async_copy(source.at[others], target.at[others], recv_sem).wait()
    pltpu.make_async_copy(source.at[others], target.at[others], send_sem).wait()


def pack(parts, staged, outgoing):
    rest = parts[0] - parts[0].astype(BF).astype(F32)
    for row, part in enumerate((*parts, rest)):
        staged[pl.ds(row, PEERS, stride=4), :] = part
    outgoing[...] = staged[...].astype(BF).reshape(PEERS, 4, 128)


def unpack(incoming, staged):
    staged[...] = incoming[...].astype(F32).reshape(PEERS * 4, 128)
    return [staged[pl.ds(row, PEERS, stride=4), :].astype(BF) for row in range(4)]


def swapped(value):
    return pltpu.roll(value, CELLS, axis=1)


WIDE = 14
SPAN = 3 * 4 * WIDE
HIDDEN = 16


def neighbours():
    return [(a, b) for a in (-1, 0, 1) for b in (-1, 0, 1) if (a, b) != (0, 0)]


def span(side, sending):
    if side == 0:
        return pl.ds(0, 8) if sending else pl.ds(3, 8)
    if side < 0:
        return pl.ds(0, 3) if sending else pl.ds(WIDE - 3, 3)
    return pl.ds(5, 3) if sending else pl.ds(0, 3)


def halo_copies(edge, around, sems):
    gy, gz = lax.axis_index("gy"), lax.axis_index("gz")
    return {
        (a, b): pltpu.make_async_remote_copy(
            edge.at[span(a, True), span(b, True)],
            around.at[span(a, False), span(b, False)],
            sems.at[index],
            sems.at[8 + index],
            device_id=shifted(a, b),
            device_id_type=MESH,
        )
        for index, (a, b) in enumerate(neighbours())
    }


def taken(cells, y, rows):
    return jnp.concatenate([cells[y, t, rows, :] for t in range(4)], axis=1)


def put(cells, y, rows, value):
    for t in range(4):
        cells[y, t, rows, :] = value[:, 128 * t : 128 * (t + 1)]


def place(velocity, cells, edge):
    def row(y, carry):
        for c in range(4):
            value = velocity[c, y] if c < 3 else jnp.zeros((8, NL), F32)
            for t in range(4):
                cells[y + 3, t, pl.ds(12 + c, 8, stride=4), :] = value[:, 128 * t : 128 * (t + 1)]
        edge[y] = taken(cells, y + 3, pl.ds(12, 32)).astype(BF).reshape(8, 4, NL)
        return carry

    lax.fori_loop(0, 8, row, 0, unroll=UNROLL_PLACE)


def bands(first, first_pick, second, second_pick, bias, first_matrix, second_rows, second_matrix, bias_rows):
    eye = lax.broadcasted_iota(jnp.int32, (HIDDEN, HIDDEN), 0) == lax.broadcasted_iota(
        jnp.int32, (HIDDEN, HIDDEN), 1
    )
    column = jnp.sum(jnp.where(eye, bias[...], 0.0), axis=1, keepdims=True)
    base = dot(first[...], first_pick[...])
    for z in range(12):
        rows = base if z == 0 else pltpu.roll(base, 4 * z, axis=1)
        first_matrix[pl.ds(HIDDEN * z, HIDDEN), :] = rows.astype(BF)
        bias_rows[pl.ds(HIDDEN * z, HIDDEN), :] = jnp.broadcast_to(column, (HIDDEN, 128))
    taps = dot(second[...], second_pick[...])
    channel = lax.broadcasted_iota(jnp.int32, (9, 256), 0)
    for a in range(3):
        near = taps[:, 256 * a : 256 * (a + 1)]
        slope = pltpu.roll(near, HIDDEN, axis=1) - pltpu.roll(near, 256 - HIDDEN, axis=1)
        value = jnp.where(lax.rem(channel, 3) == 2, slope, near)
        gap = jnp.zeros((9, 112), F32)
        base = jnp.concatenate(
            [value[:, :80], gap, value[:, 80:160], gap, value[:, 160:240], gap, gap[:, :64]], axis=1
        )
        for z in range(8):
            rows = base if z == 0 else pltpu.roll(base, HIDDEN * z, axis=1)
            for t in range(5):
                second_rows[t, pl.ds(72 * a + z, 9, stride=8), :] = rows[:, 128 * t : 128 * (t + 1)]
    second_matrix[...] = jnp.concatenate([second_rows[t, :216] for t in range(5)], axis=1)[
        :, : 36 * HIDDEN
    ].astype(BF)


def stack(cells, stacked, low, high):
    def row(y, carry):
        value = taken(cells, y, pl.ds(0, 4 * WIDE))
        at = y * SPAN
        stacked[pl.ds(pl.multiple_of(at, 8), 56), :] = pltpu.roll(value, 1, axis=1)
        stacked[pl.ds(pl.multiple_of(at + 56, 8), 56), :] = value
        stacked[pl.ds(pl.multiple_of(at + 112, 8), 56), :] = pltpu.roll(value, NL - 1, axis=1)
        return carry

    lax.fori_loop(low, high, row, 0, unroll=UNROLL_STACK)


def spread_middle(around, cells, stacked):
    def sides(y, carry):
        put(cells, y, pl.ds(0, 12), around[y, pl.ds(0, 3)].astype(F32).reshape(12, NL))
        put(cells, y, pl.ds(44, 12), around[y, pl.ds(11, 3)].astype(F32).reshape(12, NL))
        return carry

    lax.fori_loop(3, 11, sides, 0, unroll=UNROLL_STACK)
    stack(cells, stacked, 3, 11)
    stacked[pl.ds(11 * SPAN, 8), :] = jnp.zeros((8, NL), F32)


def spread_ends(around, cells, stacked):
    for y in (*range(3), *range(WIDE - 3, WIDE)):
        put(cells, y, pl.ds(0, 4 * WIDE), around[y].astype(F32).reshape(4 * WIDE, NL))
    stack(cells, stacked, 0, 3)
    stack(cells, stacked, WIDE - 3, WIDE)
    stacked[pl.ds(WIDE * SPAN, 8), :] = jnp.zeros((8, NL), F32)


def correct(bias, stacked, first_matrix, second_matrix, learned, low, high, fresh):
    def layer(y, carry):
        source = stacked[pl.ds(pl.multiple_of(y * SPAN, 8), 512), :].astype(BF)
        before = dot(first_matrix[...], source) + bias[:, :1]
        hidden = before * (0.5 + 0.5 * jnp.tanh(0.5 * before))
        wide = jnp.concatenate(
            [
                pltpu.roll(hidden, 1, axis=1).astype(BF),
                hidden.astype(BF),
                pltpu.roll(hidden, NL - 1, axis=1).astype(BF),
            ],
            axis=0,
        )
        part = dot(second_matrix[...], wide)
        if fresh:
            learned[y + 2] = part[:72]
        else:
            learned[y + 2] += part[:72]
        learned[y + 1] += part[72:144]
        learned[y] += part[144:]
        return carry

    lax.fori_loop(low, high, layer, 0, unroll=UNROLL_LAYER)


def advance(velocity, forcing, cells, learned, stepped):
    steps = (2.0 * math.pi / NL, 2.0 * math.pi / 128, 2.0 * math.pi / 128)
    half = [0.5 / h for h in steps]
    square = [1.0 / h**2 for h in steps]

    def ahead(value):
        return pltpu.roll(value, NL - 1, axis=1)

    def behind(value):
        return pltpu.roll(value, 1, axis=1)

    def lines(y, c, z):
        return taken(cells, y, pl.ds(12 + 4 * z + c, 8, stride=4))

    def move(y, carry):
        here = [velocity[c, y] for c in range(3)]
        over = [lines(y + 4, c, 0) for c in range(3)]
        under = [lines(y + 2, c, 0) for c in range(3)]
        far = [lines(y + 3, c, 1) for c in range(3)]
        near = [lines(y + 3, c, -1) for c in range(3)]
        for i in range(3):
            first = here[i] * here[0] + learned[y + 3, pl.ds(24 * i, 8), :].astype(BF).astype(F32)
            rows = pl.ds(24 * i + 8, 8)
            second = (over[i] * over[1] + learned[y + 4, rows, :]) - (
                under[i] * under[1] + learned[y + 2, rows, :]
            )
            third = (far[i] * far[2] - near[i] * near[2]) + learned[y + 3, pl.ds(24 * i + 16, 8), :]
            divergence = (
                (ahead(first) - behind(first)) * half[0] + second * half[1] + third * half[2]
            )
            twice = 2.0 * here[i]
            laplacian = (
                (ahead(here[i]) + behind(here[i]) - twice) * square[0]
                + (over[i] + under[i] - twice) * square[1]
                + (far[i] + near[i] - twice) * square[2]
            )
            stepped[i, pl.ds(pl.multiple_of(8 * y, 8), 8), :] = (
                here[i] + time_step * (viscosity * laplacian - divergence) + forcing[i, y]
            )
        return carry

    lax.fori_loop(0, 8, move, 0)


def picks():
    first = np.zeros((81, 512))
    second = np.zeros((27 * HIDDEN, 3 * 256))
    for a in range(3):
        for b in range(3):
            for e in range(3):
                for c in range(3):
                    first[c * 27 + a * 9 + b * 3 + e, (3 * a + e) * 4 * WIDE + 4 * b + c] = 1.0
                for c in range(HIDDEN):
                    row = c * 27 + a * 9 + b * 3 + e
                    lane = 80 * e + c
                    second[row, 256 * a + lane + HIDDEN * (b + 1)] = 1.0
    return first.astype(BF), second.astype(BF)


def whole(
    velocity,
    first,
    first_pick,
    bias,
    second,
    second_pick,
    forcing_far,
    *rest,
):
    (
        far_tables,
        (result, cells, edge, around, stacked, first_matrix, second_rows, second_matrix, bias_rows, learned, stepped),
        (staged, outgoing, incoming, outgoing_back, incoming_back),
        (forcing, *tables),
        (halo_sems, load_sems, sems, ready),
    ) = [rest[slice(*bounds)] for bounds in ((0, 9), (9, 20), (20, 25), (25, 35), (35, 39))]
    barrier = pltpu.get_barrier_semaphore()
    tell(barrier, 1)
    loads = [
        pltpu.make_async_copy(source, target, load_sems.at[index])
        for index, (source, target) in enumerate(zip((forcing_far, *far_tables), (forcing, *tables)))
    ]
    for load in loads:
        load.start()
    place(velocity, cells, edge)
    pl.semaphore_wait(barrier, 8)
    copies = halo_copies(edge, around, halo_sems)
    for copy in copies.values():
        copy.start()
    tell(ready.at[0], 1)
    learned[pl.ds(0, 5)] = jnp.zeros((5, 72, NL), F32)
    bands(first, first_pick, second, second_pick, bias, first_matrix, second_rows, second_matrix, bias_rows)
    copies[0, -1].wait_recv()
    copies[0, 1].wait_recv()
    pl.semaphore_wait(ready.at[0], 8)
    tell(ready.at[1], 2)
    spread_middle(around, cells, stacked)
    correct(bias_rows, stacked, first_matrix, second_matrix, learned, 3, 9, True)
    for (a, _), copy in copies.items():
        if a != 0:
            copy.wait_recv()
    pl.semaphore_wait(ready.at[1], 8)
    tell(ready.at[2], 4)
    spread_ends(around, cells, stacked)
    correct(bias_rows, stacked, first_matrix, second_matrix, learned, 9, 12, True)
    correct(bias_rows, stacked, first_matrix, second_matrix, learned, 0, 3, False)
    for load in loads:
        load.wait()
    advance(velocity, forcing, cells, learned, stepped)
    pl.semaphore_wait(ready.at[2], 8)
    for copy in copies.values():
        copy.wait_send()
    lines_high, lines_low, outer_high, outer_low, inner_high, inner_low, back_high, back_low, twiddle = tables
    gy, gz = lax.axis_index("gy"), lax.axis_index("gz")
    nt = ((1,), (1,))
    high, low = split(stepped[...].reshape(3 * CELLS, NL))
    modes = dot(lines_high[...], high, nt) + (dot(lines_low[...], high, nt) + dot(lines_high[...], low, nt))
    pack(
        [
            jnp.concatenate(
                [modes[:PEERS, CELLS * c : CELLS * (c + 1)], modes[PEERS:, CELLS * c : CELLS * (c + 1)]],
                axis=1,
            )
            for c in range(3)
        ],
        staged,
        outgoing,
    )
    exchange(outgoing, incoming, sems.at[0], sems.at[1], sems.at[2])
    rows = jnp.concatenate(unpack(incoming, staged), axis=1)
    both = dot(outer_high[...], rows) + dot(outer_low[...], rows)
    lane = lax.broadcasted_iota(jnp.int32, (PEERS, 128), 1)
    sign = jnp.where(lane < CELLS, 1.0, -1.0).astype(F32)
    spun = []
    for c in range(3):
        at = 128 * c
        upper, lower = both[:PEERS, at : at + 128], both[PEERS:, at : at + 128]
        if c == 0:
            upper, lower = upper + both[:PEERS, 384:], lower + both[PEERS:, 384:]
        value = upper + swapped(lower) * sign
        spun.append(value * twiddle[0] + swapped(value) * twiddle[1])
    high, low = split(jnp.concatenate(spun, axis=0))
    modes = dot(high, inner_high[...]) + (dot(low, inner_high[...]) + dot(high, inner_low[...]))
    slot = gy * GZ + gz
    wave_x = slot.astype(F32)
    wave_y, wave_z = signed_waves()
    squared = wave_x * wave_x + wave_y * wave_y + wave_z * wave_z
    inverse = jnp.where(squared > 0, 1.0 / jnp.maximum(squared, 1.0), 0.0)
    parts = [modes[PEERS * c : PEERS * (c + 1)] for c in range(3)]
    potential = (wave_x * parts[0] + wave_y * parts[1] + wave_z * parts[2]) * inverse
    weight = jnp.where(slot == 0, 1.0, 2.0).astype(F32) / (NL * 128.0 * 128.0)
    parts = [
        (part - wave * potential) * weight for part, wave in zip(parts, (wave_x, wave_y, wave_z))
    ]
    high, low = split(jnp.concatenate(parts, axis=0))
    near = dot(high, back_high[...]) + (dot(low, back_high[...]) + dot(high, back_low[...]))
    spun = []
    for c in range(3):
        value = near[PEERS * c : PEERS * (c + 1)]
        spun.append(value * twiddle[0] - swapped(value) * twiddle[1])
    high, low = split(jnp.concatenate(spun, axis=1))
    both = dot(outer_high[...], high) + (dot(outer_high[...], low) + dot(outer_low[...], high))
    pack(
        [
            both[:PEERS, 128 * c : 128 * (c + 1)] - swapped(both[PEERS:, 128 * c : 128 * (c + 1)]) * sign
            for c in range(3)
        ],
        staged,
        outgoing_back,
    )
    exchange(outgoing_back, incoming_back, sems.at[3], sems.at[4], sems.at[5])
    rows = [value.astype(F32) for value in unpack(incoming_back, staged)]
    real = jnp.concatenate([value[:, :CELLS] for value in rows], axis=1)
    imag = jnp.concatenate([value[:, CELLS:] for value in rows], axis=1)
    packed = jnp.concatenate([real, imag], axis=0).T.astype(BF)
    field = dot(packed, lines_high[...]) + dot(packed, lines_low[...])
    result[...] = jnp.concatenate(
        [field[:CELLS] + field[3 * CELLS :], field[CELLS : 3 * CELLS]], axis=0
    ).reshape(3, CELLS, NL)


def body(velocity, forcing, first_kernel, first_bias, second_kernel):
    tables = spectral_tables()
    first_pick, second_pick = picks()
    vmem, away = pl.BlockSpec(memory_space=pltpu.VMEM), pl.BlockSpec(memory_space=pl.ANY)
    field = pl.pallas_call(
        whole,
        out_shape=jax.ShapeDtypeStruct((3, CELLS, NL), F32),
        in_specs=[vmem] * 6 + [away] * (1 + len(tables)),
        out_specs=vmem,
        scratch_shapes=[
            pltpu.VMEM((WIDE, 4, 64, 128), F32),
            pltpu.VMEM((8, 8, 4, NL), BF),
            pltpu.VMEM((WIDE, WIDE, 4, NL), BF),
            pltpu.VMEM((WIDE * SPAN + 8, NL), F32),
            pltpu.VMEM((12 * HIDDEN, 512), BF),
            pltpu.VMEM((5, 288, 128), F32),
            pltpu.VMEM((216, 36 * HIDDEN), BF),
            pltpu.VMEM((12 * HIDDEN, 128), F32),
            pltpu.VMEM((WIDE, 72, NL), F32),
            pltpu.VMEM((3, CELLS, NL), F32),
            pltpu.VMEM((4 * PEERS, 128), F32),
            *[pltpu.VMEM((PEERS, 4, 128), BF)] * 4,
            pltpu.VMEM(forcing.shape, F32),
            *[pltpu.VMEM(table.shape, table.dtype) for table in tables],
            pltpu.SemaphoreType.DMA((16,)),
            pltpu.SemaphoreType.DMA((1 + len(tables),)),
            pltpu.SemaphoreType.DMA((6,)),
            pltpu.SemaphoreType.REGULAR((3,)),
        ],
        compiler_params=pltpu.CompilerParams(
            collective_id=0, has_side_effects=True, vmem_limit_bytes=67_000_000
        ),
    )(
        velocity,
        first_kernel.reshape(HIDDEN, 81),
        first_pick,
        first_bias.reshape(1, HIDDEN),
        second_kernel.reshape(9, 27 * HIDDEN),
        second_pick,
        forcing,
        *tables,
    )
    return field.reshape(velocity.shape)


def solution(mesh):
    placed = (P(None, "gy", "gz", None), P(None, "gy", "gz", None), P(), P(), P())
    return jax.shard_map(
        body, mesh=mesh, in_specs=placed, out_specs=P(None, "gy", "gz", None), check_vma=False
    )
```
